32 devices in a mesh: field: 4 (over y, core), tile: 8 (over z, x).
Axes of the slice: x: 2, y: 2, z: 4, core: 2. Of those that a mesh axis runs over, the one named last changes fastest.
Arguments:
- density: float32 [8, 4, 8, 128], P('tile'), may hold values from 0.8 to 1.2
- velocity: float32 [3, 8, 4, 8, 128], P(None, 'tile'), may hold values from -3 to 3
- energy: float32 [8, 4, 8, 128], P('tile'), may hold values from 0.8 to 1.2
- species: float32 [16, 16, 8, 4, 8, 128], P('field', None, 'tile'), may hold values from 0 to 1
- wiener: float32 [2, 16, 3, 8, 4, 8, 128], P(None, 'field', None, 'tile'), may hold values from -6 to 6
- substeps: int32 [8, 4, 8, 128], P('tile'), may hold values from 1 to 4
- mix_rate: float32 [8, 4, 8, 128], P('tile'), may hold values from 0.5 to 5
- reactants: float32 [96, 16], replicated, may hold values from -1.5 to 1.5
- stoich: float32 [16, 96], replicated, may hold values from -0.625 to 0.625
- kinetic_constants: float32 [96], replicated, may hold values from 0.2 to 2
- excitation_sensitivity: float32 [96], replicated, may hold values from 0.5 to 4
- heat: float32 [16], replicated, may hold values from -4 to 4
- molar: float32 [16], replicated, may hold values from 0.05 to 0.2
Outputs:
- flow_out: float32 [5, 8, 4, 8, 128], P(None, 'tile')
- species_out: float32 [16, 16, 8, 4, 8, 128], P('field', None, 'tile')
The draws below stay inside these ranges and needn't reach their ends.
All inputs are finite; a program needn't handle non-finite values.
Results may differ from the reference program's by a relative error of at most 0.0003.
Values sent between devices are 32-bit elements; how exact they have to be, the bound alone decides.
A program may use at most 64 MiB of HBM per device.

```python
import math
import jax
import jax.numpy as jnp
from jax import lax

SPECIES = 16
REACT = 96
REALIZATIONS = 16
SUBS = 4
STEPS = 2
CZ = 4
CY = 8
NX = 128
TILES = 8
TY = 8
N_TILE = 8


def touch_ends(result, rng, smallest, largest):
    shape = result.shape
    spot = [jax.random.randint(jax.random.fold_in(rng, axis), (), 0, shape[axis]) for axis in range(len(shape))]
    result = result.at[tuple(spot)].set(smallest)
    longest = shape.index(max(shape))
    spot[longest] = (spot[longest] + 1) % shape[longest]
    return result.at[tuple(spot)].set(largest)


def block_scale(rng, extent, cuts, least, top_value):
    def one(axis_at, shards_of):
        steps = jax.random.uniform(jax.random.fold_in(jax.random.fold_in(rng, 6), axis_at), (shards_of,), jnp.float32, least / len(cuts), top_value / len(cuts))
        return jnp.repeat(jnp.exp(steps), extent[axis_at] // shards_of).reshape((-1,) + (1,) * (len(extent) - axis_at - 1))

    gain = one(*cuts[0])
    for cut in cuts[1:]:
        gain = gain * one(*cut)
    return gain


def scatter_about(key, shape, width, limit, cuts=(), dtype=jnp.bfloat16):
    loudness = block_scale(key, shape, cuts, -0.22, 0.18) if cuts else 1.0
    entries = jax.random.normal(key, shape, jnp.float32) * width * loudness
    return jnp.minimum(jnp.maximum(entries, -limit), limit).astype(dtype)


def setup_inputs(seed: int = 0) -> dict:
    key_of = jax.random.split(jax.random.key(seed), 14)
    density = jnp.clip(0.8 + 0.40000004 * jax.random.uniform(key_of[0], (TILES, CZ, CY, NX), jnp.float32) ** block_scale(key_of[0], (TILES, CZ, CY, NX), ((0, 8),), -0.2, 0.2), 0.8, 1.2)
    velocity = scatter_about(key_of[1], (3, TILES, CZ, CY, NX), 0.5, 3.0, ((1, 8),), jnp.float32)
    energy = jnp.clip(0.8 + 0.40000004 * jax.random.uniform(key_of[2], (TILES, CZ, CY, NX), jnp.float32) ** block_scale(key_of[2], (TILES, CZ, CY, NX), ((0, 8),), -0.2, 0.2), 0.8, 1.2)
    species = jnp.clip(1.0 * jax.random.uniform(key_of[3], (REALIZATIONS, SPECIES, TILES, CZ, CY, NX), jnp.float32) ** block_scale(key_of[3], (REALIZATIONS, SPECIES, TILES, CZ, CY, NX), ((0, 4), (2, 8)), -0.2, 0.2), 0.0, 1.0)
    wiener = scatter_about(key_of[4], (STEPS, REALIZATIONS, 3, TILES, CZ, CY, NX), 1.0, 6.0, ((1, 4), (3, 8)), jnp.float32)
    substeps = touch_ends(jax.random.randint(key_of[5], (TILES, CZ, CY, NX), 1, SUBS + 1), jax.random.fold_in(key_of[5], 1), 1, SUBS).astype(jnp.int32)
    mix_rate = jnp.clip(jnp.exp(math.log(5.0) - 2.3025851 * jax.random.uniform(key_of[6], (TILES, CZ, CY, NX), jnp.float32) ** block_scale(key_of[6], (TILES, CZ, CY, NX), ((0, 8),), -0.2, 0.2)), 0.5, 5.0)
    reactants = scatter_about(key_of[7], (REACT, SPECIES), SPECIES ** -0.5, 1.5, (), jnp.float32)
    stoich = scatter_about(key_of[8], (SPECIES, REACT), REACT ** -0.5, 0.625, (), jnp.float32)
    kinetic_constants = jnp.clip(jnp.exp(jax.random.uniform(key_of[9], (REACT,), jnp.float32, math.log(0.2), math.log(2.0))), 0.2, 2.0)
    excitation_sensitivity = jnp.clip(jnp.exp(jax.random.uniform(key_of[10], (REACT,), jnp.float32, math.log(0.5), math.log(4.0))), 0.5, 4.0)
    heat = scatter_about(key_of[11], (SPECIES,), 1.0, 4.0, (), jnp.float32)
    molar = jnp.clip(jax.random.uniform(key_of[12], (SPECIES,), jnp.float32, 0.05, 0.2), 0.05, 0.2)
    return {"density": density, "velocity": velocity, "energy": energy, "species": species, "wiener": wiener, "substeps": substeps, "mix_rate": mix_rate, "reactants": reactants, "stoich": stoich, "kinetic_constants": kinetic_constants, "excitation_sensitivity": excitation_sensitivity, "heat": heat, "molar": molar}


time_step = 0.1
viscosity = 0.4
diffusivity = 0.3
relaxation = 2.0
noise_scale = math.sqrt(2.0 * 0.3 * 0.1)

def to_grid(blocks):
    leading = blocks.shape[:-4]
    split = blocks.reshape(leading + (N_TILE // TY, TY, CZ, CY, NX))
    return jnp.swapaxes(split, -4, -3).reshape(leading + (N_TILE // TY * CZ, TY * CY, NX))

def to_blocks(grid):
    leading = grid.shape[:-3]
    split = grid.reshape(leading + (N_TILE // TY, CZ, TY, CY, NX))
    return jnp.swapaxes(split, -4, -3).reshape(leading + (N_TILE, CZ, CY, NX))

def pad_cells(values):
    widths = [(0, 0)] * (values.ndim - 3) + [(1, 1)] * 3
    return jnp.pad(values, widths)

def neighbours(padded):
    centre = padded[..., 1:-1, 1:-1, 1:-1]
    grad_z = (padded[..., 2:, 1:-1, 1:-1] - padded[..., :-2, 1:-1, 1:-1]) * 0.5
    grad_y = (padded[..., 1:-1, 2:, 1:-1] - padded[..., 1:-1, :-2, 1:-1]) * 0.5
    grad_x = (padded[..., 1:-1, 1:-1, 2:] - padded[..., 1:-1, 1:-1, :-2]) * 0.5
    laplacian = padded[..., 2:, 1:-1, 1:-1] + padded[..., :-2, 1:-1, 1:-1]
    laplacian = laplacian + padded[..., 1:-1, 2:, 1:-1] + padded[..., 1:-1, :-2, 1:-1]
    laplacian = laplacian + padded[..., 1:-1, 1:-1, 2:] + padded[..., 1:-1, 1:-1, :-2] - 6.0 * centre
    return (centre, (grad_z, grad_y, grad_x), laplacian)

def flow_update(padded):
    centre, gradients, laplacian = neighbours(padded)
    carried = centre[1] * gradients[0] + centre[2] * gradients[1] + centre[3] * gradients[2]
    return centre + time_step * (viscosity * laplacian - carried)

def march_forward(padded, speeds, noise_draw):
    centre, gradients, laplacian = neighbours(padded)
    carried = speeds[0] * gradients[0] + speeds[1] * gradients[1] + speeds[2] * gradients[2]
    noisy = gradients[0] * noise_draw[:, 0][:, None] + gradients[1] * noise_draw[:, 1][:, None] + gradients[2] * noise_draw[:, 2][:, None]
    return centre + time_step * (diffusivity * laplacian - carried) + noise_scale * noisy

def react_field(flattened, kinetic_multiplier, sub_counts, step_len, reactants, stoich):
    for fractional_increment in range(SUBS):
        driving = jnp.dot(reactants, flattened, precision=lax.Precision.HIGHEST)
        changes = jnp.dot(stoich, kinetic_multiplier * driving, precision=lax.Precision.HIGHEST)
        flattened = flattened + jnp.where(sub_counts > fractional_increment, step_len, 0.0) * changes
    return flattened

def reference(density, velocity, energy, species, wiener, substeps, mix_rate, reactants, stoich, kinetic_constants, excitation_sensitivity, heat, molar):
    fluid_state = jnp.concatenate([to_grid(density)[None], to_grid(velocity), to_grid(energy)[None]], 0)
    species = to_grid(species)
    noise_all = to_grid(wiener)
    mix_grid = to_grid(mix_rate)
    sub_counts = to_grid(substeps).reshape(-1)
    step_len = time_step / sub_counts.astype(jnp.float32)
    number_of_cells = sub_counts.shape[0]
    for current_step_index in range(STEPS):
        fluid_state = flow_update(pad_cells(fluid_state))
        carried = march_forward(pad_cells(species), fluid_state[1:4], noise_all[current_step_index])
        field_mean = lax.optimization_barrier(jnp.sum(carried, 0)) / REALIZATIONS
        mixed = carried - time_step * mix_grid * (carried - field_mean)
        pointwise_thermal_level = fluid_state[4].reshape(-1)
        kinetic_multiplier = kinetic_constants[:, None] * jnp.exp(excitation_sensitivity[:, None] * (pointwise_thermal_level - 1.0))
        flattened = mixed.reshape(REALIZATIONS, SPECIES, number_of_cells)
        reacted = lax.map(lambda one: react_field(one, kinetic_multiplier, sub_counts, step_len, reactants, stoich), flattened)
        heat_released = lax.optimization_barrier(jnp.sum(heat[None, :, None] * (reacted - flattened), (0, 1))) / REALIZATIONS
        density_mean = lax.optimization_barrier(jnp.sum(molar[None, :, None] * reacted, (0, 1))) / REALIZATIONS
        species = reacted.reshape(species.shape)
        heat_released = heat_released.reshape(fluid_state.shape[1:])
        density_mean = density_mean.reshape(fluid_state.shape[1:])
        fluid_state = jnp.concatenate([(fluid_state[0] + time_step * relaxation * (density_mean - fluid_state[0]))[None], fluid_state[1:4], (fluid_state[4] + heat_released)[None]], 0)
    return (to_blocks(fluid_state), to_blocks(species))
```

```python
import functools
import math

import jax
import jax.numpy as jnp
from jax import lax
from jax.experimental import pallas as pl
from jax.experimental.pallas import tpu as pltpu
from jax.sharding import PartitionSpec as P

SUBS = 4

time_step = 0.1
viscosity = 0.4
diffusivity = 0.3
relaxation = 2.0
noise_scale = math.sqrt(2.0 * 0.3 * 0.1)

f32 = jnp.float32
bf16 = jnp.bfloat16


def split(value):
    high = value.astype(bf16)
    return high, (value - high.astype(f32)).astype(bf16)


def lanes(pieces):
    return pieces[0] if len(pieces) == 1 else jnp.concatenate(pieces, 1)


def column(row, count, width):
    spot = lax.broadcasted_iota(jnp.int32, (count, count), 0)
    lane = lax.broadcasted_iota(jnp.int32, (count, count), 1)
    picked = jnp.sum(jnp.where(spot == lane, row, 0.0), 1, keepdims=True)
    return jnp.broadcast_to(picked, (count, width))


def spread(value, slots):
    k = value.shape[1]
    shape = (k, len(slots) * k)
    source = lax.broadcasted_iota(jnp.int32, shape, 0)
    target = lax.broadcasted_iota(jnp.int32, shape, 1)
    where = jnp.zeros(shape, f32)
    for slot, used in enumerate(slots):
        if used:
            where = jnp.where(target == source + slot * k, 1.0, where)
    return jnp.dot(value, where.astype(bf16), preferred_element_type=f32)


def kernel(
    dims,
    density,
    velocity,
    energy,
    species,
    wiener,
    substeps,
    mix_rate,
    reactants,
    stoich,
    kinetic,
    sensitivity,
    heat,
    molar,
    flow_out,
    species_out,
    grid,
    flow,
    fresh,
    state,
    total,
    from_partner,
    chip_sum,
    from_peers,
    mean,
    mean_out,
    rates,
    step_of,
    kin,
    sens,
    heat_col,
    molar_col,
    first,
    second,
    send_sem,
    recv_sem,
):
    n_tile, n_field, fields, spc, nz, ny, nx, react, steps = dims
    realizations = fields * n_field
    half = nz // 2
    peers = n_field // 2 - 1
    tile = lax.axis_index("tile")
    field = lax.axis_index("field")
    core = lax.rem(field, 2)
    partner = field + 1 - 2 * core
    others = [lax.rem(field + 2 * (hop + 1), n_field) for hop in range(peers)]
    has_below = tile > 0
    has_above = tile < n_tile - 1
    mine = core * half
    theirs = half - mine

    barrier = pltpu.get_barrier_semaphore()

    def greet(where):
        pl.semaphore_signal(
            barrier, inc=1, device_id=where, device_id_type=pl.DeviceIdType.MESH
        )

    for other in [partner] + others:
        greet({"field": other})

    @pl.when(has_below)
    def _():
        greet({"tile": tile - 1})

    @pl.when(has_above)
    def _():
        greet({"tile": tile + 1})

    def bring_row(y):
        def one(z, carry):
            for f in range(fields):
                start = f * spc * nz * ny + z * ny + y
                grid[0, f, z + 1, y + 1] = species[pl.ds(start, spc, stride=nz * ny), :]
            flow[0, z + 1, y + 1, 0:1] = density[pl.ds(z * ny + y, 1), :]
            for i in range(3):
                flow[0, z + 1, y + 1, 1 + i : 2 + i] = velocity[
                    pl.ds((i * nz + z) * ny + y, 1), :
                ]
            flow[0, z + 1, y + 1, 4:5] = energy[pl.ds(z * ny + y, 1), :]
            flow[0, z + 1, y + 1, 5:8] = jnp.zeros((3, nx), f32)
            return carry

        lax.fori_loop(0, nz, one, 0)

    bring_row(0)
    bring_row(ny - 1)

    near = (tile + n_tile - 1) // n_tile + (2 * n_tile - 2 - tile) // n_tile
    pl.semaphore_wait(barrier, 1 + peers + near)

    def remote(source, target, slot, where):
        return pltpu.make_async_remote_copy(
            src_ref=source,
            dst_ref=target,
            send_sem=send_sem.at[slot],
            recv_sem=recv_sem.at[slot],
            device_id=where,
            device_id_type=pl.DeviceIdType.MESH,
        )

    per_step = 6 + peers

    def halo_copies(t):
        base = t * per_step
        inner = pl.ds(1, nz)
        up = [
            remote(grid.at[t, :, inner, ny], grid.at[t, :, inner, 0], base, {"tile": tile + 1}),
            remote(flow.at[t, inner, ny], flow.at[t, inner, 0], base + 1, {"tile": tile + 1}),
        ]
        down = [
            remote(grid.at[t, :, inner, 1], grid.at[t, :, inner, ny + 1], base + 2, {"tile": tile - 1}),
            remote(flow.at[t, inner, 1], flow.at[t, inner, ny + 1], base + 3, {"tile": tile - 1}),
        ]
        return up, down

    def halo_start(t):
        up, down = halo_copies(t)

        @pl.when(has_above)
        def _():
            for copy in reversed(up):
                copy.start()

        @pl.when(has_below)
        def _():
            for copy in reversed(down):
                copy.start()

    def halo_wait(t):
        up, down = halo_copies(t)

        @pl.when(has_below)
        def _():
            for copy in up:
                copy.wait_recv()

        @pl.when(has_above)
        def _():
            for copy in down:
                copy.wait_recv()

    def halo_sent(t):
        up, down = halo_copies(t)

        @pl.when(has_above)
        def _():
            for copy in up:
                copy.wait_send()

        @pl.when(has_below)
        def _():
            for copy in down:
                copy.wait_send()

    halo_start(0)

    for y in range(1, ny - 1):
        bring_row(y)

    blank = jnp.zeros((spc, nx), f32)
    for t in range(steps):
        for z in (0, nz + 1):
            for y in range(ny + 2):
                for f in range(fields):
                    grid[t, f, z, y] = blank
                flow[t, z, y] = jnp.zeros((8, nx), f32)

        def blank_row(y):
            for z in range(1, nz + 1):
                for f in range(fields):
                    grid[t, f, z, y] = blank
                flow[t, z, y] = jnp.zeros((8, nx), f32)

        @pl.when(jnp.logical_not(has_below))
        def _():
            blank_row(0)

        @pl.when(jnp.logical_not(has_above))
        def _():
            blank_row(ny + 1)

    kin[...] = column(kinetic[...], react, nx)
    sens[...] = column(sensitivity[...], react, nx)
    heat_col[...] = column(heat[...], spc, nx)
    molar_col[...] = column(molar[...], spc, nx)
    r_high, r_low = split(reactants[...])
    first[...] = (spread(r_high, (1, 0, 1)) + spread(r_low, (0, 1, 0))).astype(bf16)
    s_high, s_low = split(stoich[...])
    second[0:spc] = spread(s_high, (1, 1)).astype(bf16)
    second[spc : 2 * spc] = spread(s_low, (1, 1)).astype(bf16)

    lane_at = lax.broadcasted_iota(jnp.int32, (1, nx), 1)
    not_last = jnp.where(lane_at < nx - 1, 1.0, 0.0)
    not_first = jnp.where(lane_at > 0, 1.0, 0.0)

    def stencil(ref, z, y, weight, slopes):
        centre = ref[z + 1, y + 1]
        out = centre * (1.0 - 6.0 * weight)
        out += (weight + slopes[0]) * ref[z + 2, y + 1] + (weight - slopes[0]) * ref[z, y + 1]
        out += (weight + slopes[1]) * ref[z + 1, y + 2] + (weight - slopes[1]) * ref[z + 1, y]
        out += ((weight + slopes[2]) * not_last) * pltpu.roll(centre, nx - 1, 1)
        out += ((weight - slopes[2]) * not_first) * pltpu.roll(centre, 1, 1)
        return out

    def advance(t, ys):
        def one(z, carry):
            for y in ys:
                old = flow.at[t]
                speeds = [flow[t, z + 1, y + 1, 1 + i : 2 + i] for i in range(3)]
                moved = stencil(
                    old, z, y, time_step * viscosity, [-0.5 * time_step * u for u in speeds]
                )
                fresh[z, y] = moved
                summed = None
                for f in range(fields):
                    slopes = []
                    for i in range(3):
                        at = (((t * fields + f) * 3 + i) * nz + z) * ny + y
                        noise = wiener[pl.ds(at, 1), :]
                        slopes.append(
                            (0.5 * noise_scale) * noise - (0.5 * time_step) * moved[1 + i : 2 + i]
                        )
                    carried = stencil(grid.at[t, f], z, y, time_step * diffusivity, slopes)
                    state[f, z, y] = carried
                    summed = carried if summed is None else summed + carried
                total[t, z, y] = summed
            return carry

        lax.fori_loop(0, nz, one, 0)

    def substep(values, multiplier, steps_at):
        for k in range(SUBS):
            high, low = split(values)
            driving = jnp.dot(
                first[...], jnp.concatenate([high, high, low], 0), preferred_element_type=f32
            )
            high, low = split(multiplier * driving)
            both = jnp.dot(
                second[...], jnp.concatenate([high, low], 0), preferred_element_type=f32
            )
            values = values + steps_at(k) * (both[:spc] + both[spc:])
        return values

    def lengths(z, y, k):
        counts = substeps[pl.ds(z * ny + y, 1), :]
        return jnp.where(counts > k, time_step / counts.astype(f32), 0.0)

    def chemistry(ys, z_from, z_to):
        def one(z, carry):
            results = []
            for y in ys:
                level = fresh[z, y, 4:5] - 1.0
                rate = kin[...] * jnp.exp(sens[...] * level)
                rates[z, y] = rate
                values = lanes([state[f, z, y] for f in range(fields)])
                results.append(
                    substep(
                        values,
                        lanes([rate] * fields),
                        lambda k, y=y: lanes([lengths(z, y, k)] * fields),
                    )
                )
            for y, result in zip(ys, results):
                for f in range(fields):
                    state[f, z, y] = result[:, f * nx : (f + 1) * nx]
            return carry

        lax.fori_loop(z_from, z_to, one, 0)

    group = 4

    def mean_chemistry(t):
        def one(z, carry):
            at = mine + z
            results = []
            for y0 in range(0, ny, group):
                ys = range(y0, min(y0 + group, ny))
                values = lanes([mean[z, y] for y in ys])
                result = substep(
                    values,
                    lanes([rates[at, y] for y in ys]),
                    lambda k, ys=ys: lanes([lengths(at, y, k) for y in ys]),
                )
                gained = jnp.sum(lanes([heat_col[...]] * len(ys)) * (result - values), 0, keepdims=True)
                dense = jnp.sum(lanes([molar_col[...]] * len(ys)) * result, 0, keepdims=True)
                results.append((ys, result, gained, dense))
            for ys, result, gained, dense in results:
                for j, y in enumerate(ys):
                    piece = slice(j * nx, (j + 1) * nx)
                    mean_out[t, at, y, 0:spc] = result[:, piece]
                    mean_out[t, at, y, spc : spc + 1] = dense[:, piece]
                    mean_out[t, at, y, spc + 1 : spc + 2] = gained[:, piece]
                    mean_out[t, at, y, spc + 2 : spc + 8] = jnp.zeros((6, nx), f32)
            return carry

        lax.fori_loop(0, half, one, 0)

    def combine(t, ys):
        last = t == steps - 1

        def one(z, carry):
            for y in ys:
                share = time_step * mix_rate[pl.ds(z * ny + y, 1), :]
                settled = share * mean_out[t, z, y, 0:spc]
                for f in range(fields):
                    value = (1.0 - share) * state[f, z, y] + settled
                    if last:
                        start = f * spc * nz * ny + z * ny + y
                        species_out[pl.ds(start, spc, stride=nz * ny), :] = value
                    else:
                        grid[t + 1, f, z + 1, y + 1] = value
                held = fresh[z, y, 0:1]
                dense = held + (time_step * relaxation) * (mean_out[t, z, y, spc : spc + 1] - held)
                hot = fresh[z, y, 4:5] + mean_out[t, z, y, spc + 1 : spc + 2]
                if last:
                    flow_out[pl.ds(z * ny + y, 1), :] = dense
                    for i in range(1, 4):
                        flow_out[pl.ds((i * nz + z) * ny + y, 1), :] = fresh[z, y, i : i + 1]
                    flow_out[pl.ds((4 * nz + z) * ny + y, 1), :] = hot
                else:
                    flow[t + 1, z + 1, y + 1] = fresh[z, y]
                    flow[t + 1, z + 1, y + 1, 0:1] = dense
                    flow[t + 1, z + 1, y + 1, 4:5] = hot
            return carry

        lax.fori_loop(0, nz, one, 0)

    inside = list(range(1, ny - 1))
    edges = [0, ny - 1]
    for t in range(steps):
        base = t * per_step
        advance(t, inside)
        chemistry(inside, 0, half)
        halo_wait(t)
        advance(t, edges)
        to_partner = remote(
            total.at[t, pl.ds(theirs, half)], from_partner.at[t], base + 4, {"field": partner}
        )
        to_partner.start()
        chemistry(edges, 0, half)
        to_partner.wait_recv()
        for z in range(half):
            chip_sum[t, z] = total[t, mine + z] + from_partner[t, z]
        to_peers = [
            remote(chip_sum.at[t], from_peers.at[t, hop], base + 6 + hop, {"field": other})
            for hop, other in enumerate(others)
        ]
        for copy in to_peers:
            copy.start()
        chemistry(inside, half, nz)
        chemistry(edges, half, nz)
        for copy in to_peers:
            copy.wait_recv()
        for z in range(half):
            whole = chip_sum[t, z]
            for hop in range(peers):
                whole = whole + from_peers[t, hop, z]
            mean[z] = whole * (1.0 / realizations)
        mean_chemistry(t)
        back = remote(
            mean_out.at[t, pl.ds(mine, half)],
            mean_out.at[t, pl.ds(mine, half)],
            base + 5,
            {"field": partner},
        )
        back.start()
        back.wait_recv()
        combine(t, edges)
        if t + 1 < steps:
            halo_start(t + 1)
        combine(t, inside)
        halo_sent(t)
        to_partner.wait_send()
        for copy in to_peers:
            copy.wait_send()
        back.wait_send()


def solution(mesh):
    n_tile, n_field = mesh.shape["tile"], mesh.shape["field"]

    def on_device(
        density,
        velocity,
        energy,
        species,
        wiener,
        substeps,
        mix_rate,
        reactants,
        stoich,
        kinetic_constants,
        excitation_sensitivity,
        heat,
        molar,
    ):
        fields, spc, _, nz, ny, nx = species.shape
        steps = wiener.shape[0]
        react = reactants.shape[0]
        peers = n_field // 2 - 1
        dims = (n_tile, n_field, fields, spc, nz, ny, nx, react, steps)
        half = nz // 2
        copies = steps * (6 + peers)
        vmem = pl.BlockSpec(memory_space=pltpu.VMEM)
        flow_out, species_out = pl.pallas_call(
            functools.partial(kernel, dims),
            out_shape=(
                jax.ShapeDtypeStruct((5 * nz * ny, nx), f32),
                jax.ShapeDtypeStruct((fields * spc * nz * ny, nx), f32),
            ),
            in_specs=[vmem] * 13,
            out_specs=(vmem, vmem),
            scratch_shapes=[
                pltpu.VMEM((steps, fields, nz + 2, ny + 2, spc, nx), f32),
                pltpu.VMEM((steps, nz + 2, ny + 2, 8, nx), f32),
                pltpu.VMEM((nz, ny, 8, nx), f32),
                pltpu.VMEM((fields, nz, ny, spc, nx), f32),
                pltpu.VMEM((steps, nz, ny, spc, nx), f32),
                pltpu.VMEM((steps, half, ny, spc, nx), f32),
                pltpu.VMEM((steps, half, ny, spc, nx), f32),
                pltpu.VMEM((steps, max(peers, 1), half, ny, spc, nx), f32),
                pltpu.VMEM((half, ny, spc, nx), f32),
                pltpu.VMEM((steps, nz, ny, spc + 8, nx), f32),
                pltpu.VMEM((nz, ny, react, nx), f32),
                pltpu.VMEM((8, nx), f32),
                pltpu.VMEM((react, nx), f32),
                pltpu.VMEM((react, nx), f32),
                pltpu.VMEM((spc, nx), f32),
                pltpu.VMEM((spc, nx), f32),
                pltpu.VMEM((react, 3 * spc), bf16),
                pltpu.VMEM((2 * spc, 2 * react), bf16),
                pltpu.SemaphoreType.DMA((copies,)),
                pltpu.SemaphoreType.DMA((copies,)),
            ],
            compiler_params=pltpu.CompilerParams(
                collective_id=0, has_side_effects=True, vmem_limit_bytes=60000 * 1024
            ),
        )(
            density.reshape(nz * ny, nx),
            velocity.reshape(3 * nz * ny, nx),
            energy.reshape(nz * ny, nx),
            species.reshape(fields * spc * nz * ny, nx),
            wiener.reshape(steps * fields * 3 * nz * ny, nx),
            substeps.reshape(nz * ny, nx),
            mix_rate.reshape(nz * ny, nx),
            reactants,
            stoich,
            kinetic_constants.reshape(1, react),
            excitation_sensitivity.reshape(1, react),
            heat.reshape(1, spc),
            molar.reshape(1, spc),
        )
        return (
            flow_out.reshape(5, 1, nz, ny, nx),
            species_out.reshape(fields, spc, 1, nz, ny, nx),
        )

    placed = (
        P("tile", None, None, None),
        P(None, "tile", None, None, None),
        P("tile", None, None, None),
        P("field", None, "tile", None, None, None),
        P(None, "field", None, "tile", None, None, None),
        P("tile", None, None, None),
        P("tile", None, None, None),
        P(),
        P(),
        P(),
        P(),
        P(),
        P(),
    )
    return jax.shard_map(
        on_device,
        mesh=mesh,
        in_specs=placed,
        out_specs=(P(None, "tile", None, None, None), P("field", None, "tile", None, None, None)),
        check_vma=False,
    )
```

```python
import functools
import math

import jax
import jax.numpy as jnp
from jax import lax
from jax.experimental import pallas as pl
from jax.experimental.pallas import tpu as pltpu
from jax.sharding import PartitionSpec as P

SUBS = 4
LAG = (1, 2)
CHAIN = 2

time_step = 0.1
viscosity = 0.4
diffusivity = 0.3
relaxation = 2.0
noise_scale = math.sqrt(2.0 * 0.3 * 0.1)

f32 = jnp.float32
bf16 = jnp.bfloat16


def split(value):
    high = value.astype(bf16)
    return high, (value - high.astype(f32)).astype(bf16)


def lanes(pieces):
    return pieces[0] if len(pieces) == 1 else jnp.concatenate(pieces, 1)


def column(row, count, width):
    spot = lax.broadcasted_iota(jnp.int32, (count, count), 0)
    lane = lax.broadcasted_iota(jnp.int32, (count, count), 1)
    picked = jnp.sum(jnp.where(spot == lane, row, 0.0), 1, keepdims=True)
    return jnp.broadcast_to(picked, (count, width))


def spread(value, slots):
    k = value.shape[1]
    shape = (k, len(slots) * k)
    source = lax.broadcasted_iota(jnp.int32, shape, 0)
    target = lax.broadcasted_iota(jnp.int32, shape, 1)
    where = jnp.zeros(shape, f32)
    for slot, used in enumerate(slots):
        if used:
            where = jnp.where(target == source + slot * k, 1.0, where)
    return jnp.dot(value, where.astype(bf16), preferred_element_type=f32)


def kernel(
    dims,
    density,
    velocity,
    energy,
    species,
    wiener,
    substeps,
    mix_rate,
    reactants,
    stoich,
    kinetic,
    sensitivity,
    heat,
    molar,
    flow_out,
    species_out,
    grid,
    flow,
    fresh,
    state,
    total,
    from_partner,
    chip_sum,
    from_peers,
    mean,
    mean_out,
    rates,
    step_of,
    kin,
    sens,
    heat_col,
    molar_col,
    first,
    second,
    send_sem,
    recv_sem,
):
    n_tile, n_field, fields, spc, nz, ny, nx, react, steps = dims
    realizations = fields * n_field
    half = nz // 2
    peers = n_field // 2 - 1
    tile = lax.axis_index("tile")
    field = lax.axis_index("field")
    core = lax.rem(field, 2)
    partner = field + 1 - 2 * core
    others = [lax.rem(field + 2 * (hop + 1), n_field) for hop in range(peers)]
    has_below = tile > 0
    has_above = tile < n_tile - 1
    mine = core * half
    theirs = half - mine

    barrier = pltpu.get_barrier_semaphore()

    def greet(where):
        pl.semaphore_signal(
            barrier, inc=1, device_id=where, device_id_type=pl.DeviceIdType.MESH
        )

    for other in [partner] + others:
        greet({"field": other})

    @pl.when(has_below)
    def _():
        greet({"tile": tile - 1})

    @pl.when(has_above)
    def _():
        greet({"tile": tile + 1})

    def bring_row(y):
        def one(z, carry):
            for f in range(fields):
                start = f * spc * nz * ny + z * ny + y
                grid[0, f, z + 1, y + 1] = species[pl.ds(start, spc, stride=nz * ny), :]
            flow[0, z + 1, y + 1, 0:1] = density[pl.ds(z * ny + y, 1), :]
            for i in range(3):
                flow[0, z + 1, y + 1, 1 + i : 2 + i] = velocity[
                    pl.ds((i * nz + z) * ny + y, 1), :
                ]
            flow[0, z + 1, y + 1, 4:5] = energy[pl.ds(z * ny + y, 1), :]
            flow[0, z + 1, y + 1, 5:8] = jnp.zeros((3, nx), f32)
            return carry

        lax.fori_loop(0, nz, one, 0)

    bring_row(0)
    bring_row(ny - 1)

    near = (tile + n_tile - 1) // n_tile + (2 * n_tile - 2 - tile) // n_tile
    pl.semaphore_wait(barrier, 1 + peers + near)

    def remote(source, target, slot, where):
        return pltpu.make_async_remote_copy(
            src_ref=source,
            dst_ref=target,
            send_sem=send_sem.at[slot],
            recv_sem=recv_sem.at[slot],
            device_id=where,
            device_id_type=pl.DeviceIdType.MESH,
        )

    per_step = 6 + peers

    def halo_copies(t):
        base = t * per_step
        inner = pl.ds(1, nz)
        up = [
            remote(grid.at[t, :, inner, ny], grid.at[t, :, inner, 0], base, {"tile": tile + 1}),
            remote(flow.at[t, inner, ny], flow.at[t, inner, 0], base + 1, {"tile": tile + 1}),
        ]
        down = [
            remote(grid.at[t, :, inner, 1], grid.at[t, :, inner, ny + 1], base + 2, {"tile": tile - 1}),
            remote(flow.at[t, inner, 1], flow.at[t, inner, ny + 1], base + 3, {"tile": tile - 1}),
        ]
        return up, down

    def halo_start(t):
        up, down = halo_copies(t)

        @pl.when(has_above)
        def _():
            for copy in reversed(up):
                copy.start()

        @pl.when(has_below)
        def _():
            for copy in reversed(down):
                copy.start()

    def halo_wait(t):
        up, down = halo_copies(t)

        @pl.when(has_below)
        def _():
            for copy in up:
                copy.wait_recv()

        @pl.when(has_above)
        def _():
            for copy in down:
                copy.wait_recv()

    def halo_sent(t):
        up, down = halo_copies(t)

        @pl.when(has_above)
        def _():
            for copy in up:
                copy.wait_send()

        @pl.when(has_below)
        def _():
            for copy in down:
                copy.wait_send()

    halo_start(0)

    for y in range(1, ny - 1):
        bring_row(y)

    blank = jnp.zeros((spc, nx), f32)
    for t in range(steps):
        for z in (0, nz + 1):
            for y in range(ny + 2):
                for f in range(fields):
                    grid[t, f, z, y] = blank
                flow[t, z, y] = jnp.zeros((8, nx), f32)

        def blank_row(y):
            for z in range(1, nz + 1):
                for f in range(fields):
                    grid[t, f, z, y] = blank
                flow[t, z, y] = jnp.zeros((8, nx), f32)

        @pl.when(jnp.logical_not(has_below))
        def _():
            blank_row(0)

        @pl.when(jnp.logical_not(has_above))
        def _():
            blank_row(ny + 1)

    kin[...] = column(kinetic[...], react, nx)
    sens[...] = column(sensitivity[...], react, nx)
    heat_col[...] = column(heat[...], spc, nx)
    mean_out[...] = jnp.zeros_like(mean_out)
    molar_col[...] = column(molar[...], spc, nx)
    r_high, r_low = split(reactants[...])
    first[...] = (spread(r_high, (1, 0, 1)) + spread(r_low, (0, 1, 0))).astype(bf16)
    s_high, s_low = split(stoich[...])
    second[0:spc] = spread(s_high, (1, 1)).astype(bf16)
    second[spc : 2 * spc] = spread(s_low, (1, 1)).astype(bf16)

    lane_at = lax.broadcasted_iota(jnp.int32, (1, nx), 1)
    not_last = jnp.where(lane_at < nx - 1, 1.0, 0.0)
    not_first = jnp.where(lane_at > 0, 1.0, 0.0)

    def stencil(ref, z, y, weight, slopes):
        centre = ref[z + 1, y + 1]
        out = centre * (1.0 - 6.0 * weight)
        out += (weight + slopes[0]) * ref[z + 2, y + 1] + (weight - slopes[0]) * ref[z, y + 1]
        out += (weight + slopes[1]) * ref[z + 1, y + 2] + (weight - slopes[1]) * ref[z + 1, y]
        out += ((weight + slopes[2]) * not_last) * pltpu.roll(centre, nx - 1, 1)
        out += ((weight - slopes[2]) * not_first) * pltpu.roll(centre, 1, 1)
        return out

    def advance(t, ys):
        def one(z, carry):
            for y in ys:
                old = flow.at[t]
                speeds = [flow[t, z + 1, y + 1, 1 + i : 2 + i] for i in range(3)]
                moved = stencil(
                    old, z, y, time_step * viscosity, [-0.5 * time_step * u for u in speeds]
                )
                fresh[z, y] = moved
                summed = None
                for f in range(fields):
                    slopes = []
                    for i in range(3):
                        at = (((t * fields + f) * 3 + i) * nz + z) * ny + y
                        noise = wiener[pl.ds(at, 1), :]
                        slopes.append(
                            (0.5 * noise_scale) * noise - (0.5 * time_step) * moved[1 + i : 2 + i]
                        )
                    carried = stencil(grid.at[t, f], z, y, time_step * diffusivity, slopes)
                    state[f, z, y] = carried
                    summed = carried if summed is None else summed + carried
                total[t, z, y] = summed
            return carry

        lax.fori_loop(0, nz, one, 0)

    def substeps_of(values, multiplier_of, length_of):
        order = [(k, i) for k in range(SUBS) for i in range(len(values))]
        driving, changes = {}, {}
        for slot in range(len(order) + LAG[1]):
            if slot < len(order):
                k, i = order[slot]
                high, low = split(values[i])
                driving[slot] = jnp.dot(
                    first[...], jnp.concatenate([high, high, low], 0), preferred_element_type=f32
                )
            at = slot - LAG[0]
            if at in driving:
                high, low = split(multiplier_of(order[at][1]) * driving.pop(at))
                changes[at] = jnp.dot(
                    second[...], jnp.concatenate([high, low], 0), preferred_element_type=f32
                )
            at = slot - LAG[1]
            if at in changes:
                k, i = order[at]
                both = changes.pop(at)
                values[i] = values[i] + length_of(i, k) * (both[:spc] + both[spc:])
        return values

    def lengths(z, y, k):
        counts = substeps[pl.ds(z * ny + y, 1), :]
        return jnp.where(counts > k, time_step / counts.astype(f32), 0.0)

    def chemistry(ys, z_from, z_to, width=1):
        def one(at, carry):
            places = [(z_from + at * width + z, y) for z in range(width) for y in ys]
            for z, y in places:
                level = fresh[z, y, 4:5] - 1.0
                rates[z, y] = kin[...] * jnp.exp(sens[...] * level)
            chains = [(z, y, f) for z, y in places for f in range(0, fields, CHAIN)]

            def multiplier_of(i):
                z, y, _ = chains[i]
                return lanes([rates[z, y]] * CHAIN)

            def length_of(i, k):
                z, y, _ = chains[i]
                return lanes([lengths(z, y, k)] * CHAIN)

            values = [lanes([state[f + j, z, y] for j in range(CHAIN)]) for z, y, f in chains]
            values = substeps_of(values, multiplier_of, length_of)
            for (z, y, f), result in zip(chains, values):
                for j in range(CHAIN):
                    state[f + j, z, y] = result[:, j * nx : (j + 1) * nx]
            return carry

        lax.fori_loop(0, (z_to - z_from) // width, one, 0)

    def mean_chemistry(t):
        places = [(z, y) for z in range(half) for y in range(ny)]
        chains = [places[i : i + CHAIN] for i in range(0, len(places), CHAIN)]

        def multiplier_of(i):
            return lanes([rates[mine + z, y] for z, y in chains[i]])

        def length_of(i, k):
            return lanes([lengths(mine + z, y, k) for z, y in chains[i]])

        values = [lanes([mean[z, y] for z, y in chain]) for chain in chains]
        values = substeps_of(values, multiplier_of, length_of)
        for chain, reacted in zip(chains, values):
            for j, (z, y) in enumerate(chain):
                result = reacted[:, j * nx : (j + 1) * nx]
                at = mine + z
                mean_out[t, at, y, 0:spc] = result
                mean_out[t, at, y, spc : spc + 1] = jnp.sum(molar_col[...] * result, 0, keepdims=True)
                mean_out[t, at, y, spc + 1 : spc + 2] = jnp.sum(
                    heat_col[...] * (result - mean[z, y]), 0, keepdims=True
                )

    def combine(t, ys):
        last = t == steps - 1

        def one(z, carry):
            for y in ys:
                share = time_step * mix_rate[pl.ds(z * ny + y, 1), :]
                settled = share * mean_out[t, z, y, 0:spc]
                for f in range(fields):
                    value = (1.0 - share) * state[f, z, y] + settled
                    if last:
                        start = f * spc * nz * ny + z * ny + y
                        species_out[pl.ds(start, spc, stride=nz * ny), :] = value
                    else:
                        grid[t + 1, f, z + 1, y + 1] = value
                held = fresh[z, y, 0:1]
                dense = held + (time_step * relaxation) * (mean_out[t, z, y, spc : spc + 1] - held)
                hot = fresh[z, y, 4:5] + mean_out[t, z, y, spc + 1 : spc + 2]
                if last:
                    flow_out[pl.ds(z * ny + y, 1), :] = dense
                    for i in range(1, 4):
                        flow_out[pl.ds((i * nz + z) * ny + y, 1), :] = fresh[z, y, i : i + 1]
                    flow_out[pl.ds((4 * nz + z) * ny + y, 1), :] = hot
                else:
                    flow[t + 1, z + 1, y + 1] = fresh[z, y]
                    flow[t + 1, z + 1, y + 1, 0:1] = dense
                    flow[t + 1, z + 1, y + 1, 4:5] = hot
            return carry

        lax.fori_loop(0, nz, one, 0)

    inside = list(range(1, ny - 1))
    edges = [0, ny - 1]
    for t in range(steps):
        base = t * per_step
        advance(t, inside)
        chemistry(inside, 0, half)
        halo_wait(t)
        advance(t, edges)
        to_partner = remote(
            total.at[t, pl.ds(theirs, half)], from_partner.at[t], base + 4, {"field": partner}
        )
        to_partner.start()
        chemistry(edges, 0, half, half)
        to_partner.wait_recv()
        for z in range(half):
            chip_sum[t, z] = total[t, mine + z] + from_partner[t, z]
        to_peers = [
            remote(chip_sum.at[t], from_peers.at[t, hop], base + 6 + hop, {"field": other})
            for hop, other in enumerate(others)
        ]
        for copy in to_peers:
            copy.start()
        chemistry(list(range(ny)), half, nz)
        for copy in to_peers:
            copy.wait_recv()
        for z in range(half):
            whole = chip_sum[t, z]
            for hop in range(peers):
                whole = whole + from_peers[t, hop, z]
            mean[z] = whole * (1.0 / realizations)
        mean_chemistry(t)
        back = remote(
            mean_out.at[t, pl.ds(mine, half)],
            mean_out.at[t, pl.ds(mine, half)],
            base + 5,
            {"field": partner},
        )
        back.start()
        back.wait_recv()
        combine(t, edges)
        if t + 1 < steps:
            halo_start(t + 1)
        combine(t, inside)
        halo_sent(t)
        to_partner.wait_send()
        for copy in to_peers:
            copy.wait_send()
        back.wait_send()


def solution(mesh):
    n_tile, n_field = mesh.shape["tile"], mesh.shape["field"]

    def on_device(
        density,
        velocity,
        energy,
        species,
        wiener,
        substeps,
        mix_rate,
        reactants,
        stoich,
        kinetic_constants,
        excitation_sensitivity,
        heat,
        molar,
    ):
        fields, spc, _, nz, ny, nx = species.shape
        steps = wiener.shape[0]
        react = reactants.shape[0]
        peers = n_field // 2 - 1
        dims = (n_tile, n_field, fields, spc, nz, ny, nx, react, steps)
        half = nz // 2
        copies = steps * (6 + peers)
        vmem = pl.BlockSpec(memory_space=pltpu.VMEM)
        flow_out, species_out = pl.pallas_call(
            functools.partial(kernel, dims),
            out_shape=(
                jax.ShapeDtypeStruct((5 * nz * ny, nx), f32),
                jax.ShapeDtypeStruct((fields * spc * nz * ny, nx), f32),
            ),
            in_specs=[vmem] * 13,
            out_specs=(vmem, vmem),
            scratch_shapes=[
                pltpu.VMEM((steps, fields, nz + 2, ny + 2, spc, nx), f32),
                pltpu.VMEM((steps, nz + 2, ny + 2, 8, nx), f32),
                pltpu.VMEM((nz, ny, 8, nx), f32),
                pltpu.VMEM((fields, nz, ny, spc, nx), f32),
                pltpu.VMEM((steps, nz, ny, spc, nx), f32),
                pltpu.VMEM((steps, half, ny, spc, nx), f32),
                pltpu.VMEM((steps, half, ny, spc, nx), f32),
                pltpu.VMEM((steps, max(peers, 1), half, ny, spc, nx), f32),
                pltpu.VMEM((half, ny, spc, nx), f32),
                pltpu.VMEM((steps, nz, ny, spc + 8, nx), f32),
                pltpu.VMEM((nz, ny, react, nx), f32),
                pltpu.VMEM((8, nx), f32),
                pltpu.VMEM((react, nx), f32),
                pltpu.VMEM((react, nx), f32),
                pltpu.VMEM((spc, nx), f32),
                pltpu.VMEM((spc, nx), f32),
                pltpu.VMEM((react, 3 * spc), bf16),
                pltpu.VMEM((2 * spc, 2 * react), bf16),
                pltpu.SemaphoreType.DMA((copies,)),
                pltpu.SemaphoreType.DMA((copies,)),
            ],
            compiler_params=pltpu.CompilerParams(
                collective_id=0, has_side_effects=True, vmem_limit_bytes=60000 * 1024
            ),
        )(
            density.reshape(nz * ny, nx),
            velocity.reshape(3 * nz * ny, nx),
            energy.reshape(nz * ny, nx),
            species.reshape(fields * spc * nz * ny, nx),
            wiener.reshape(steps * fields * 3 * nz * ny, nx),
            substeps.reshape(nz * ny, nx),
            mix_rate.reshape(nz * ny, nx),
            reactants,
            stoich,
            kinetic_constants.reshape(1, react),
            excitation_sensitivity.reshape(1, react),
            heat.reshape(1, spc),
            molar.reshape(1, spc),
        )
        return (
            flow_out.reshape(5, 1, nz, ny, nx),
            species_out.reshape(fields, spc, 1, nz, ny, nx),
        )

    placed = (
        P("tile", None, None, None),
        P(None, "tile", None, None, None),
        P("tile", None, None, None),
        P("field", None, "tile", None, None, None),
        P(None, "field", None, "tile", None, None, None),
        P("tile", None, None, None),
        P("tile", None, None, None),
        P(),
        P(),
        P(),
        P(),
        P(),
        P(),
    )
    return jax.shard_map(
        on_device,
        mesh=mesh,
        in_specs=placed,
        out_specs=(P(None, "tile", None, None, None), P("field", None, "tile", None, None, None)),
        check_vma=False,
    )
```

```python
import functools
import math

import jax
import jax.numpy as jnp
from jax import lax
from jax.experimental import pallas as pl
from jax.experimental.pallas import tpu as pltpu
from jax.sharding import PartitionSpec as P

SUBS = 4
LAG = (1, 2)
CHAIN = 2

time_step = 0.1
viscosity = 0.4
diffusivity = 0.3
relaxation = 2.0
noise_scale = math.sqrt(2.0 * 0.3 * 0.1)

f32 = jnp.float32
bf16 = jnp.bfloat16


def split(value):
    high = value.astype(bf16)
    return high, (value - high.astype(f32)).astype(bf16)


def lanes(pieces):
    return pieces[0] if len(pieces) == 1 else jnp.concatenate(pieces, 1)


def column(row, count, width):
    spot = lax.broadcasted_iota(jnp.int32, (count, count), 0)
    lane = lax.broadcasted_iota(jnp.int32, (count, count), 1)
    picked = jnp.sum(jnp.where(spot == lane, row, 0.0), 1, keepdims=True)
    return jnp.broadcast_to(picked, (count, width))


def spread(value, slots, turned=0):
    k = value.shape[1 - turned]
    shape = (k, len(slots) * k)
    source = lax.broadcasted_iota(jnp.int32, shape, 0)
    target = lax.broadcasted_iota(jnp.int32, shape, 1)
    where = jnp.zeros(shape, f32)
    for slot, used in enumerate(slots):
        if used:
            where = jnp.where(target == source + slot * k, 1.0, where)
    return lax.dot_general(
        value, where.astype(bf16), (((1 - turned,), (0,)), ((), ())), preferred_element_type=f32
    )


def kernel(
    dims,
    density,
    velocity,
    energy,
    species,
    wiener,
    substeps,
    mix_rate,
    reactants,
    stoich,
    kinetic,
    sensitivity,
    heat,
    molar,
    flow_out,
    species_out,
    grid,
    flow,
    fresh,
    state,
    total,
    from_partner,
    chip_sum,
    from_peers,
    mean,
    mean_out,
    rates,
    step_of,
    kin,
    sens,
    heat_col,
    molar_col,
    first,
    second,
    send_sem,
    recv_sem,
):
    n_tile, n_field, fields, spc, nz, ny, nx, react, steps = dims
    realizations = fields * n_field
    half = nz // 2
    peers = n_field // 2 - 1
    tile = lax.axis_index("tile")
    field = lax.axis_index("field")
    core = lax.rem(field, 2)
    partner = field + 1 - 2 * core
    others = [lax.rem(field + 2 * (hop + 1), n_field) for hop in range(peers)]
    has_below = tile > 0
    has_above = tile < n_tile - 1
    mine = core * half
    theirs = half - mine

    barrier = pltpu.get_barrier_semaphore()

    def greet(where):
        pl.semaphore_signal(
            barrier, inc=1, device_id=where, device_id_type=pl.DeviceIdType.MESH
        )

    for other in [partner] + others:
        greet({"field": other})

    @pl.when(has_below)
    def _():
        greet({"tile": tile - 1})

    @pl.when(has_above)
    def _():
        greet({"tile": tile + 1})

    def bring_row(y):
        def one(z, carry):
            for f in range(fields):
                start = f * spc * nz * ny + z * ny + y
                grid[0, f, z + 1, y + 1] = species[pl.ds(start, spc, stride=nz * ny), :]
            flow[0, z + 1, y + 1, 0:1] = density[pl.ds(z * ny + y, 1), :]
            for i in range(3):
                flow[0, z + 1, y + 1, 1 + i : 2 + i] = velocity[
                    pl.ds((i * nz + z) * ny + y, 1), :
                ]
            flow[0, z + 1, y + 1, 4:5] = energy[pl.ds(z * ny + y, 1), :]
            flow[0, z + 1, y + 1, 5:8] = jnp.zeros((3, nx), f32)
            return carry

        lax.fori_loop(0, nz, one, 0)

    bring_row(0)
    bring_row(ny - 1)

    near = (tile + n_tile - 1) // n_tile + (2 * n_tile - 2 - tile) // n_tile
    pl.semaphore_wait(barrier, 1 + peers + near)

    def remote(source, target, slot, where):
        return pltpu.make_async_remote_copy(
            src_ref=source,
            dst_ref=target,
            send_sem=send_sem.at[slot],
            recv_sem=recv_sem.at[slot],
            device_id=where,
            device_id_type=pl.DeviceIdType.MESH,
        )

    per_step = 6 + peers

    def halo_copies(t):
        base = t * per_step
        inner = pl.ds(1, nz)
        up = [
            remote(grid.at[t, :, inner, ny], grid.at[t, :, inner, 0], base, {"tile": tile + 1}),
            remote(flow.at[t, inner, ny], flow.at[t, inner, 0], base + 1, {"tile": tile + 1}),
        ]
        down = [
            remote(grid.at[t, :, inner, 1], grid.at[t, :, inner, ny + 1], base + 2, {"tile": tile - 1}),
            remote(flow.at[t, inner, 1], flow.at[t, inner, ny + 1], base + 3, {"tile": tile - 1}),
        ]
        return up, down

    def halo_start(t):
        up, down = halo_copies(t)

        @pl.when(has_above)
        def _():
            for copy in reversed(up):
                copy.start()

        @pl.when(has_below)
        def _():
            for copy in reversed(down):
                copy.start()

    def halo_wait(t):
        up, down = halo_copies(t)

        @pl.when(has_below)
        def _():
            for copy in up:
                copy.wait_recv()

        @pl.when(has_above)
        def _():
            for copy in down:
                copy.wait_recv()

    def halo_sent(t):
        up, down = halo_copies(t)

        @pl.when(has_above)
        def _():
            for copy in up:
                copy.wait_send()

        @pl.when(has_below)
        def _():
            for copy in down:
                copy.wait_send()

    halo_start(0)

    for y in range(1, ny - 1):
        bring_row(y)

    blank = jnp.zeros((spc, nx), f32)
    for t in range(steps):
        for z in (0, nz + 1):
            for y in range(ny + 2):
                for f in range(fields):
                    grid[t, f, z, y] = blank
                flow[t, z, y] = jnp.zeros((8, nx), f32)

        def blank_row(y):
            for z in range(1, nz + 1):
                for f in range(fields):
                    grid[t, f, z, y] = blank
                flow[t, z, y] = jnp.zeros((8, nx), f32)

        @pl.when(jnp.logical_not(has_below))
        def _():
            blank_row(0)

        @pl.when(jnp.logical_not(has_above))
        def _():
            blank_row(ny + 1)

    kin[...] = column(kinetic[...], react, nx)
    sens[...] = column(sensitivity[...], react, nx)
    heat_col[...] = column(heat[...], spc, nx)
    mean_out[...] = jnp.zeros_like(mean_out)
    molar_col[...] = column(molar[...], spc, nx)
    r_high, r_low = split(reactants[...])
    first[...] = (spread(r_high, (1, 0, 1), 1) + spread(r_low, (0, 1, 0), 1)).astype(bf16)
    s_high, s_low = split(stoich[...])
    second[0:spc] = spread(s_high, (1, 1)).astype(bf16)
    second[spc : 2 * spc] = spread(s_low, (1, 1)).astype(bf16)

    lane_at = lax.broadcasted_iota(jnp.int32, (1, nx), 1)
    not_last = jnp.where(lane_at < nx - 1, 1.0, 0.0)
    not_first = jnp.where(lane_at > 0, 1.0, 0.0)

    def stencil(ref, z, y, weight, slopes):
        centre = ref[z + 1, y + 1]
        out = centre * (1.0 - 6.0 * weight)
        out += (weight + slopes[0]) * ref[z + 2, y + 1] + (weight - slopes[0]) * ref[z, y + 1]
        out += (weight + slopes[1]) * ref[z + 1, y + 2] + (weight - slopes[1]) * ref[z + 1, y]
        out += ((weight + slopes[2]) * not_last) * pltpu.roll(centre, nx - 1, 1)
        out += ((weight - slopes[2]) * not_first) * pltpu.roll(centre, 1, 1)
        return out

    def advance(t, ys):
        def one(z, carry):
            for y in ys:
                old = flow.at[t]
                speeds = [flow[t, z + 1, y + 1, 1 + i : 2 + i] for i in range(3)]
                moved = stencil(
                    old, z, y, time_step * viscosity, [-0.5 * time_step * u for u in speeds]
                )
                fresh[z, y] = moved
                summed = None
                for f in range(fields):
                    slopes = []
                    for i in range(3):
                        at = (((t * fields + f) * 3 + i) * nz + z) * ny + y
                        noise = wiener[pl.ds(at, 1), :]
                        slopes.append(
                            (0.5 * noise_scale) * noise - (0.5 * time_step) * moved[1 + i : 2 + i]
                        )
                    carried = stencil(grid.at[t, f], z, y, time_step * diffusivity, slopes)
                    state[f, z, y] = carried
                    summed = carried if summed is None else summed + carried
                total[t, z, y] = summed
            return carry

        lax.fori_loop(0, nz, one, 0)

    def substeps_of(values, multiplier_of, length_of):
        order = [(k, i) for k in range(SUBS) for i in range(len(values))]
        driving, changes = {}, {}
        for slot in range(len(order) + LAG[1]):
            if slot < len(order):
                k, i = order[slot]
                high, low = split(values[i])
                driving[slot] = jnp.dot(
                    first[...], jnp.concatenate([high, high, low], 0), preferred_element_type=f32
                )
            at = slot - LAG[0]
            if at in driving:
                high, low = split(multiplier_of(order[at][1]) * driving.pop(at))
                changes[at] = jnp.dot(
                    second[...], jnp.concatenate([high, low], 0), preferred_element_type=f32
                )
            at = slot - LAG[1]
            if at in changes:
                k, i = order[at]
                both = changes.pop(at)
                values[i] = values[i] + length_of(i, k) * (both[:spc] + both[spc:])
        return values

    def lengths(z, y, k):
        counts = substeps[pl.ds(z * ny + y, 1), :]
        return jnp.where(counts > k, time_step / counts.astype(f32), 0.0)

    def chemistry(ys, z_from, z_to, width=1):
        def one(at, carry):
            places = [(z_from + at * width + z, y) for z in range(width) for y in ys]
            for z, y in places:
                level = fresh[z, y, 4:5] - 1.0
                rates[z, y] = kin[...] * jnp.exp(sens[...] * level)
            chains = [(z, y, f) for z, y in places for f in range(0, fields, CHAIN)]

            def multiplier_of(i):
                z, y, _ = chains[i]
                return lanes([rates[z, y]] * CHAIN)

            def length_of(i, k):
                z, y, _ = chains[i]
                return lanes([lengths(z, y, k)] * CHAIN)

            values = [lanes([state[f + j, z, y] for j in range(CHAIN)]) for z, y, f in chains]
            values = substeps_of(values, multiplier_of, length_of)
            for (z, y, f), result in zip(chains, values):
                for j in range(CHAIN):
                    state[f + j, z, y] = result[:, j * nx : (j + 1) * nx]
            return carry

        lax.fori_loop(0, (z_to - z_from) // width, one, 0)

    def mean_chemistry(t):
        places = [(z, y) for z in range(half) for y in range(ny)]
        chains = [places[i : i + CHAIN] for i in range(0, len(places), CHAIN)]

        def multiplier_of(i):
            return lanes([rates[mine + z, y] for z, y in chains[i]])

        def length_of(i, k):
            return lanes([lengths(mine + z, y, k) for z, y in chains[i]])

        values = [lanes([mean[z, y] for z, y in chain]) for chain in chains]
        values = substeps_of(values, multiplier_of, length_of)
        for chain, reacted in zip(chains, values):
            for j, (z, y) in enumerate(chain):
                result = reacted[:, j * nx : (j + 1) * nx]
                at = mine + z
                mean_out[t, at, y, 0:spc] = result
                mean_out[t, at, y, spc : spc + 1] = jnp.sum(molar_col[...] * result, 0, keepdims=True)
                mean_out[t, at, y, spc + 1 : spc + 2] = jnp.sum(
                    heat_col[...] * (result - mean[z, y]), 0, keepdims=True
                )

    def combine(t, ys):
        last = t == steps - 1

        def one(z, carry):
            for y in ys:
                share = time_step * mix_rate[pl.ds(z * ny + y, 1), :]
                settled = share * mean_out[t, z, y, 0:spc]
                for f in range(fields):
                    value = (1.0 - share) * state[f, z, y] + settled
                    if last:
                        start = f * spc * nz * ny + z * ny + y
                        species_out[pl.ds(start, spc, stride=nz * ny), :] = value
                    else:
                        grid[t + 1, f, z + 1, y + 1] = value
                held = fresh[z, y, 0:1]
                dense = held + (time_step * relaxation) * (mean_out[t, z, y, spc : spc + 1] - held)
                hot = fresh[z, y, 4:5] + mean_out[t, z, y, spc + 1 : spc + 2]
                if last:
                    flow_out[pl.ds(z * ny + y, 1), :] = dense
                    for i in range(1, 4):
                        flow_out[pl.ds((i * nz + z) * ny + y, 1), :] = fresh[z, y, i : i + 1]
                    flow_out[pl.ds((4 * nz + z) * ny + y, 1), :] = hot
                else:
                    flow[t + 1, z + 1, y + 1] = fresh[z, y]
                    flow[t + 1, z + 1, y + 1, 0:1] = dense
                    flow[t + 1, z + 1, y + 1, 4:5] = hot
            return carry

        lax.fori_loop(0, nz, one, 0)

    inside = list(range(1, ny - 1))
    edges = [0, ny - 1]
    for t in range(steps):
        base = t * per_step
        advance(t, inside)
        chemistry(inside, 0, half)
        halo_wait(t)
        advance(t, edges)
        to_partner = remote(
            total.at[t, pl.ds(theirs, half)], from_partner.at[t], base + 4, {"field": partner}
        )
        to_partner.start()
        chemistry(edges, 0, half, half)
        to_partner.wait_recv()
        for z in range(half):
            chip_sum[t, z] = total[t, mine + z] + from_partner[t, z]
        to_peers = [
            remote(chip_sum.at[t], from_peers.at[t, hop], base + 6 + hop, {"field": other})
            for hop, other in enumerate(others)
        ]
        for copy in to_peers:
            copy.start()
        chemistry(list(range(ny)), half, nz)
        for copy in to_peers:
            copy.wait_recv()
        for z in range(half):
            whole = chip_sum[t, z]
            for hop in range(peers):
                whole = whole + from_peers[t, hop, z]
            mean[z] = whole * (1.0 / realizations)
        mean_chemistry(t)
        back = remote(
            mean_out.at[t, pl.ds(mine, half)],
            mean_out.at[t, pl.ds(mine, half)],
            base + 5,
            {"field": partner},
        )
        back.start()
        back.wait_recv()
        combine(t, edges)
        if t + 1 < steps:
            halo_start(t + 1)
        combine(t, inside)
        halo_sent(t)
        to_partner.wait_send()
        for copy in to_peers:
            copy.wait_send()
        back.wait_send()


def solution(mesh):
    n_tile, n_field = mesh.shape["tile"], mesh.shape["field"]

    def on_device(
        density,
        velocity,
        energy,
        species,
        wiener,
        substeps,
        mix_rate,
        reactants,
        stoich,
        kinetic_constants,
        excitation_sensitivity,
        heat,
        molar,
    ):
        fields, spc, _, nz, ny, nx = species.shape
        steps = wiener.shape[0]
        react = reactants.shape[0]
        peers = n_field // 2 - 1
        dims = (n_tile, n_field, fields, spc, nz, ny, nx, react, steps)
        half = nz // 2
        copies = steps * (6 + peers)
        vmem = pl.BlockSpec(memory_space=pltpu.VMEM)
        flow_out, species_out = pl.pallas_call(
            functools.partial(kernel, dims),
            out_shape=(
                jax.ShapeDtypeStruct((5 * nz * ny, nx), f32),
                jax.ShapeDtypeStruct((fields * spc * nz * ny, nx), f32),
            ),
            in_specs=[vmem] * 13,
            out_specs=(vmem, vmem),
            scratch_shapes=[
                pltpu.VMEM((steps, fields, nz + 2, ny + 2, spc, nx), f32),
                pltpu.VMEM((steps, nz + 2, ny + 2, 8, nx), f32),
                pltpu.VMEM((nz, ny, 8, nx), f32),
                pltpu.VMEM((fields, nz, ny, spc, nx), f32),
                pltpu.VMEM((steps, nz, ny, spc, nx), f32),
                pltpu.VMEM((steps, half, ny, spc, nx), f32),
                pltpu.VMEM((steps, half, ny, spc, nx), f32),
                pltpu.VMEM((steps, max(peers, 1), half, ny, spc, nx), f32),
                pltpu.VMEM((half, ny, spc, nx), f32),
                pltpu.VMEM((steps, nz, ny, spc + 8, nx), f32),
                pltpu.VMEM((nz, ny, react, nx), f32),
                pltpu.VMEM((8, nx), f32),
                pltpu.VMEM((react, nx), f32),
                pltpu.VMEM((react, nx), f32),
                pltpu.VMEM((spc, nx), f32),
                pltpu.VMEM((spc, nx), f32),
                pltpu.VMEM((react, 3 * spc), bf16),
                pltpu.VMEM((2 * spc, 2 * react), bf16),
                pltpu.SemaphoreType.DMA((copies,)),
                pltpu.SemaphoreType.DMA((copies,)),
            ],
            compiler_params=pltpu.CompilerParams(
                collective_id=0, has_side_effects=True, vmem_limit_bytes=60000 * 1024
            ),
        )(
            density.reshape(nz * ny, nx),
            velocity.reshape(3 * nz * ny, nx),
            energy.reshape(nz * ny, nx),
            species.reshape(fields * spc * nz * ny, nx),
            wiener.reshape(steps * fields * 3 * nz * ny, nx),
            substeps.reshape(nz * ny, nx),
            mix_rate.reshape(nz * ny, nx),
            reactants.T,
            stoich,
            kinetic_constants.reshape(1, react),
            excitation_sensitivity.reshape(1, react),
            heat.reshape(1, spc),
            molar.reshape(1, spc),
        )
        return (
            flow_out.reshape(5, 1, nz, ny, nx),
            species_out.reshape(fields, spc, 1, nz, ny, nx),
        )

    placed = (
        P("tile", None, None, None),
        P(None, "tile", None, None, None),
        P("tile", None, None, None),
        P("field", None, "tile", None, None, None),
        P(None, "field", None, "tile", None, None, None),
        P("tile", None, None, None),
        P("tile", None, None, None),
        P(),
        P(),
        P(),
        P(),
        P(),
        P(),
    )
    return jax.shard_map(
        on_device,
        mesh=mesh,
        in_specs=placed,
        out_specs=(P(None, "tile", None, None, None), P("field", None, "tile", None, None, None)),
        check_vma=False,
    )
```
